512 devices in a mesh: slab: 4 (over x), cout: 8 (over y), cin: 16 (over z, core).
Axes of the slice: x: 4, y: 8, z: 8, core: 2. Of those that a mesh axis runs over, the one named last changes fastest.
Arguments:
- image_in: float32 [32, 64, 2048], P('slab', None, 'cin'), may hold values from -6 to 6
- first_weight: float32 [3, 3, 2048, 2048], P(None, None, 'cin', 'cout'), may hold values from -0.046875 to 0.046875
- second_weight: float32 [3, 3, 2048, 2048], P(None, None, 'cout', 'cin'), may hold values from -0.046875 to 0.046875
- out_grad: float32 [32, 64, 2048], P('slab', None, 'cin'), may hold values from -0.13258252 to 0.13258252
Outputs:
- output: float32 [32, 64, 2048], P('slab', 'cout', 'cin')
- weight_grad: float32 [3, 3, 2048, 2048], P(None, None, ('cout', 'slab'), 'cin')
The draws below stay inside these ranges and needn't reach their ends.
All inputs are finite; a program needn't handle non-finite values.
Results may differ from the reference program's by a relative error of at most 0.0001.
Values sent between devices are 32-bit elements; how exact they have to be, the bound alone decides.
No kernel may reach another device: no remote copies, remote signals or barrier semaphores. Data moves between devices by JAX's collectives and lax.ppermute only.
A program may use at most 64 MiB of HBM per device.

```python
import jax
import jax.numpy as jnp
from jax import lax

C = 2048
WIDTH = 64
ROWS_DEV = 8
HEIGHT = 32
N_SLAB = 4


def shard_levels(rng, dims, pieces, low, top_value):
    gain = 1.0
    for axis_at, parts in pieces:
        draws = jax.random.uniform(jax.random.fold_in(jax.random.fold_in(rng, 6), axis_at), (parts,), jnp.float32, low / len(pieces), top_value / len(pieces))
        gain = gain * jnp.repeat(jnp.exp(draws), dims[axis_at] // parts).reshape((-1,) + (1,) * (len(dims) - 1 - axis_at))
    return gain


def noise(rng, shape, width, limit, split=(), dtype=jnp.bfloat16):
    result = width * jax.random.normal(rng, shape, jnp.float32)
    if split:
        result = result * shard_levels(rng, shape, split, -0.22, 0.18)
    return jnp.clip(result, -limit, limit).astype(dtype)


def setup_inputs(seed: int = 0) -> dict:
    arg_keys = jax.random.split(jax.random.key(seed), 5)
    return {
        "image_in": noise(arg_keys[0], (HEIGHT, WIDTH, C), 1.0, 6.0, ((0, 4), (2, 16)), jnp.float32),
        "first_weight": noise(arg_keys[1], (3, 3, C, C), (9 * C) ** -0.5, 0.046875, ((2, 16), (3, 8)), jnp.float32),
        "second_weight": noise(arg_keys[2], (3, 3, C, C), (9 * C) ** -0.5, 0.046875, ((2, 8), (3, 16)), jnp.float32),
        "out_grad": noise(arg_keys[3], (HEIGHT, WIDTH, C), (1.0 / (ROWS_DEV * N_SLAB * WIDTH) ** 0.5), 0.13258252, ((0, 4), (2, 16)), jnp.float32),
    }


def conv_taps(padded, weight, row_count, col_count):
    summed = jnp.zeros((row_count * col_count, weight.shape[3]), jnp.float32)
    for row_off in range(3):
        for col_off in range(3):
            window = padded[row_off:row_off + row_count, col_off:col_off + col_count, :].reshape(row_count * col_count, -1)
            summed = summed + jnp.dot(window, weight[row_off, col_off], precision=lax.Precision.HIGHEST, preferred_element_type=jnp.float32)
    return summed.reshape(row_count, col_count, -1)


def reference(image_in, first_weight, second_weight, out_grad):
    row_count = image_in.shape[0]
    col_count = image_in.shape[1]
    padded = jnp.pad(image_in, ((1, 1), (1, 1), (0, 0)))
    hidden = jax.nn.silu(conv_taps(padded, first_weight, row_count, col_count))
    hidden_pad = jnp.pad(hidden, ((1, 1), (1, 1), (0, 0)))
    output = conv_taps(hidden_pad, second_weight, row_count, col_count)
    flat_grad = out_grad.reshape(row_count * col_count, -1)
    grads = []
    for row_off in range(3):
        for col_off in range(3):
            window = hidden_pad[row_off:row_off + row_count, col_off:col_off + col_count, :].reshape(row_count * col_count, -1)
            grads.append(lax.dot_general(window, flat_grad, (((0,), (0,)), ((), ())), precision=lax.Precision.HIGHEST, preferred_element_type=jnp.float32))
    weight_grad = jnp.stack(grads).reshape(3, 3, hidden.shape[2], flat_grad.shape[1])
    return output, weight_grad
```

```python
import jax
import jax.numpy as jnp
from jax import lax
from jax.sharding import PartitionSpec as P

HIGH = lax.Precision.HIGH


def shift(value, axis, step, wrap):
    count = lax.axis_size(axis)
    pairs = [(i, (i + step) % count) for i in range(count) if wrap or 0 <= i + step < count]
    return lax.ppermute(value, axis, pairs)


def conv_taps(padded, weight, row_count, col_count):
    summed = None
    for row_off in range(3):
        for col_off in range(3):
            window = padded[
                row_off : row_off + row_count, col_off : col_off + col_count, :
            ].reshape(row_count * col_count, -1)
            part = jnp.dot(
                window,
                weight[row_off, col_off],
                precision=HIGH,
                preferred_element_type=jnp.float32,
            )
            summed = part if summed is None else summed + part
    return summed


def on_device(image_in, first_weight, second_weight, out_grad):
    rows, cols = image_in.shape[0], image_in.shape[1]
    slabs, n_in, n_out = lax.axis_size("slab"), lax.axis_size("cin"), lax.axis_size("cout")
    slab = lax.axis_index("slab")
    ext_rows = rows + 2

    above = shift(image_in[rows - 2 :], "slab", 1, False)
    below = shift(image_in[:2], "slab", -1, False)
    image_ext = jnp.concatenate([above, image_in, below], axis=0)
    padded = jnp.pad(image_ext, ((0, 0), (1, 1), (0, 0)))
    partial_value = conv_taps(padded, first_weight, ext_rows, cols)

    mid = partial_value.shape[1]
    chunk = ext_rows * cols // n_in
    pieces = lax.all_to_all(
        partial_value.reshape(n_in, chunk, mid), "cin", 0, 0, tiled=True
    )
    own = jax.nn.silu(jnp.sum(pieces, axis=0))
    hidden_ext = lax.all_gather(own, "cin", axis=0, tiled=True).reshape(ext_rows, cols, mid)
    row_at = slab * rows - 1 + jnp.arange(ext_rows)
    inside = (row_at >= 0) & (row_at < slabs * rows)
    hidden_ext = jnp.where(inside[:, None, None], hidden_ext, 0.0)
    hidden_pad = jnp.pad(hidden_ext, ((0, 0), (1, 1), (0, 0)))

    flat_grad = out_grad.reshape(rows * cols, -1)
    grads = []
    for row_off in range(3):
        for col_off in range(3):
            window = hidden_pad[
                row_off : row_off + rows, col_off : col_off + cols, :
            ].reshape(rows * cols, -1)
            grads.append(
                lax.dot_general(
                    window,
                    flat_grad,
                    (((0,), (0,)), ((), ())),
                    precision=HIGH,
                    preferred_element_type=jnp.float32,
                )
            )
    local_grad = jnp.stack(grads)
    part = mid // slabs
    kept = lax.dynamic_slice_in_dim(local_grad, slab * part, part, axis=1)
    for step in range(1, slabs):
        sent = lax.dynamic_slice_in_dim(
            local_grad, lax.rem(slab + step, slabs) * part, part, axis=1
        )
        kept = kept + shift(sent, "slab", step, True)
    weight_grad = kept.reshape(3, 3, part, flat_grad.shape[1])

    second_part = conv_taps(hidden_pad, second_weight, rows, cols)
    second_part = second_part.reshape(rows, n_out, cols // n_out, -1).transpose(1, 0, 2, 3)
    gathered = lax.all_to_all(second_part, "cout", 0, 0, tiled=True)
    output = jnp.sum(gathered, axis=0)
    return (output, weight_grad)


def solution(mesh):
    in_specs = (
        P("slab", None, "cin"),
        P(None, None, "cin", "cout"),
        P(None, None, "cout", "cin"),
        P("slab", None, "cin"),
    )
    out_specs = (P("slab", "cout", "cin"), P(None, None, ("cout", "slab"), "cin"))
    return jax.shard_map(
        on_device, mesh=mesh, in_specs=in_specs, out_specs=out_specs, check_vma=False
    )
```

```python
import functools

import jax
import jax.numpy as jnp
from jax import lax
from jax.experimental import pallas as pl
from jax.experimental.pallas import tpu as pltpu
from jax.sharding import PartitionSpec as P


F32, BF16 = jnp.float32, jnp.bfloat16
VMEM = pl.BlockSpec(memory_space=pltpu.VMEM)
ANY = pl.BlockSpec(memory_space=pl.ANY)
SMEM = pl.BlockSpec(memory_space=pltpu.SMEM)
CORES = 2
LIMIT = pltpu.CompilerParams(vmem_limit_bytes=24 * 2**20)


def near(value):
    return pltpu.with_memory_space_constraint(value, pltpu.VMEM)


def shift(value, axis, step):
    count = lax.axis_size(axis)
    pairs = [(i, i + step) for i in range(count) if 0 <= i + step < count]
    return lax.ppermute(value, axis, pairs)


def turn(value, axis, step):
    count = lax.axis_size(axis)
    return lax.ppermute(value, axis, [(i, (i + step) % count) for i in range(count)])


def split(value):
    high = value.astype(BF16)
    return high, (value - high.astype(F32)).astype(BF16)


def dot(left, right):
    return jnp.dot(left, right, preferred_element_type=F32)


def taps_of_row(row):
    count = row.shape[0]
    at = lax.broadcasted_iota(jnp.int32, row.shape, 0)
    left = jnp.where(at == 0, 0.0, pltpu.roll(row, 1, 0))
    right = jnp.where(at == count - 1, 0.0, pltpu.roll(row, count - 1, 0))
    return left, row, right


def store_taps(row, high, low, start):
    rows, width = row.shape
    for tap, value in enumerate(taps_of_row(row)):
        top, rest = split(value)
        high[start : start + rows, tap * width : (tap + 1) * width] = top
        low[start : start + rows, tap * width : (tap + 1) * width] = rest


def first_prepare(image, weight, high, low, w_high, w_low, image_at, weight_at, sems):
    fetch_image = pltpu.make_async_copy(image, image_at, sems.at[0])
    fetch_weight = pltpu.make_async_copy(weight, weight_at, sems.at[1])
    fetch_image.start()
    fetch_weight.start()
    fetch_image.wait()
    rows, cols, depth = image_at.shape
    for row in range(rows):
        store_taps(image_at[row], high, low, row * cols)
    fetch_weight.wait()
    for tap in range(9):
        top, rest = split(weight_at[tap])
        w_high[tap // 3, (tap % 3) * depth : (tap % 3 + 1) * depth, :] = top
        w_low[tap // 3, (tap % 3) * depth : (tap % 3 + 1) * depth, :] = rest


def half_conv(out, part, cols, high, low, w_high, w_low):
    half = out.shape[0]
    total = None
    for a in range(3):
        rows = pl.ds(pl.multiple_of(part * half + a * cols, cols), half)
        term = dot(high[rows, :], w_high[a])
        term += dot(low[rows, :], w_high[a])
        term += dot(high[rows, :], w_low[a])
        total = term if total is None else total + term
    out[...] = total


def first_given(core, above, below, high_in, low_in, w_high, w_low, given, high, low):
    edge, cols, _ = above.shape
    inner = high_in.shape[0]
    high[edge * cols : edge * cols + inner, :] = high_in[...]
    low[edge * cols : edge * cols + inner, :] = low_in[...]
    for row in range(edge):
        store_taps(above[row], high, low, row * cols)
        store_taps(below[row], high, low, (edge + row) * cols + inner)
    half_conv(given, 1 - core[0], cols, high, low, w_high, w_low)


def first_held(cols, core, high, low, w_high, w_low, held):
    half_conv(held, core[0], cols, high, low, w_high, w_low)


def prepare(weight, grad, w_pair, grad_t):
    depth, wide = weight.shape[1], weight.shape[2]
    for tap in range(9):
        top, rest = split(weight[tap])
        w_pair[tap // 3, (tap % 3) * depth : (tap % 3 + 1) * depth, :wide] = top
        w_pair[tap // 3, (tap % 3) * depth : (tap % 3 + 1) * depth, wide:] = rest
    top, rest = split(grad[...].T)
    grad_t[:wide, :] = top
    grad_t[wide:, :] = rest


def second_conv(slab, hidden, w_from, grad_from, conv, *rest):
    *local, ordered, high, low, turned, w_pair, grad_t, sems = rest
    fetch_grad = pltpu.make_async_copy(grad_from, grad_t, sems.at[0])
    fetch_w = pltpu.make_async_copy(w_from, w_pair, sems.at[1])
    fetch_grad.start()
    fetch_w.start()
    n_in, chunk, depth = hidden.shape
    chips = n_in // CORES
    n_out, rows, width, wide = conv.shape
    cols = n_out * width
    for core in range(CORES):
        for chip in range(chips):
            start = (core * chips + chip) * chunk
            ordered[start : start + chunk, :] = hidden[chip * CORES + core]
    for row in range(rows + 2):
        store_taps(ordered[row * cols : (row + 1) * cols, :], high, low, row * cols)
    slabs = len(local)
    part = local[0].shape[1]
    mine = slab[0]
    pixels = rows * cols
    fetch_grad.wait()
    for a in range(3):
        window = slice(a * cols, a * cols + pixels)
        for b in range(3):
            lanes = slice(b * depth, (b + 1) * depth)
            both = dot(grad_t[...], high[window, lanes])
            total = both[:wide] + both[wide:] + dot(grad_t[:wide, :], low[window, lanes])
            turned[...] = total.T
            for step in range(slabs):
                start = pl.multiple_of(lax.rem(mine + step, slabs) * part, part)
                local[step][a * 3 + b] = turned[pl.ds(start, part), :]
    fetch_w.wait()
    main = None
    other = None
    for a in range(3):
        window = slice(a * cols, a * cols + pixels)
        one = dot(high[window, :], w_pair[a])
        two = dot(low[window, :], w_pair[a, :, :wide])
        main = one if main is None else main + one
        other = two if other is None else other + two
    total = main[:, :wide] + main[:, wide:] + other
    for row in range(rows):
        for block in range(n_out):
            start = row * cols + block * width
            conv[block, row] = total[start : start + width, :]


def block(image_in, first_weight, second_weight, out_grad):
    rows, cols, depth = image_in.shape
    mid = first_weight.shape[3]
    wide = second_weight.shape[3]
    slabs, n_in, n_out = lax.axis_size("slab"), lax.axis_size("cin"), lax.axis_size("cout")
    slab, at = lax.axis_index("slab"), lax.axis_index("cin")
    chips = n_in // CORES
    core = lax.rem(at, CORES)
    ext = (rows + 2) * cols
    half = ext // CORES
    chunk = ext // n_in

    above = shift(image_in[rows - 2 :], "slab", 1)
    below = shift(image_in[:2], "slab", -1)
    weights = [pltpu.VMEM((3, 3 * depth, mid), BF16)] * 2
    inner = [pltpu.VMEM((rows * cols, 3 * depth), BF16)] * 2
    outer = [pltpu.VMEM(((rows + 4) * cols, 3 * depth), BF16)] * 2
    *image_parts, w_high, w_low = pl.pallas_call(
        first_prepare,
        out_shape=inner + weights,
        in_specs=[ANY] * 2,
        out_specs=[VMEM] * 4,
        scratch_shapes=[
            pltpu.VMEM((rows, cols, depth), F32),
            pltpu.VMEM((9, depth, mid), F32),
            pltpu.SemaphoreType.DMA((2,)),
        ],
        name="first_prepare",
        compiler_params=LIMIT,
    )(image_in, first_weight.reshape(9, depth, mid))
    given, high, low = pl.pallas_call(
        first_given,
        out_shape=[pltpu.VMEM((half, mid), F32)] + outer,
        in_specs=[SMEM] + [VMEM] * 6,
        out_specs=[VMEM] * 3,
        name="first_given",
        compiler_params=LIMIT,
    )(core[None], *map(near, (above, below, *image_parts, w_high, w_low)))
    held = pl.pallas_call(
        functools.partial(first_held, cols),
        out_shape=pltpu.VMEM((half, mid), F32),
        in_specs=[SMEM] + [VMEM] * 4,
        out_specs=VMEM,
        name="first_held",
        compiler_params=LIMIT,
    )(core[None], *map(near, (high, low, w_high, w_low)))

    w_pair, grad_t = pl.pallas_call(
        prepare,
        out_shape=[
            jax.ShapeDtypeStruct((3, 3 * mid, 2 * wide), BF16),
            jax.ShapeDtypeStruct((2 * wide, rows * cols), BF16),
        ],
        in_specs=[VMEM] * 2,
        out_specs=[VMEM] * 2,
        name="prepare",
        compiler_params=LIMIT,
    )(second_weight.reshape(9, mid, wide), out_grad.reshape(rows * cols, wide))

    mate = [(i, i ^ 1) for i in range(n_in)]
    held = held + lax.ppermute(given, "cin", mate)
    groups = [[CORES * z + c for z in range(chips)] for c in range(CORES)]
    pieces = lax.all_to_all(
        held.reshape(chips, chunk, mid), "cin", 0, 0, tiled=True, axis_index_groups=groups
    )
    pixel = (core * chips + at // CORES) * chunk + jnp.arange(chunk)
    row_at = slab * rows - 1 + pixel // cols
    inside = (row_at >= 0) & (row_at < slabs * rows)
    own = jnp.where(inside[:, None], jax.nn.silu(jnp.sum(pieces, axis=0)), 0.0)
    hidden = lax.all_gather(own, "cin", axis=0, tiled=False)

    conv, kept, *sent = pl.pallas_call(
        second_conv,
        out_shape=[pltpu.VMEM((n_out, rows, cols // n_out, wide), F32)]
        + [pltpu.VMEM((9, mid // slabs, wide), F32)] * slabs,
        in_specs=[SMEM, VMEM, ANY, ANY],
        out_specs=[VMEM] * (1 + slabs),
        scratch_shapes=[
            pltpu.VMEM((ext, mid), F32),
            pltpu.VMEM((ext, 3 * mid), BF16),
            pltpu.VMEM((ext, 3 * mid), BF16),
            pltpu.VMEM((mid, wide), F32),
            pltpu.VMEM((3, 3 * mid, 2 * wide), BF16),
            pltpu.VMEM((2 * wide, rows * cols), BF16),
            pltpu.SemaphoreType.DMA((2,)),
        ],
        name="second_conv",
        compiler_params=LIMIT,
    )(slab[None], near(hidden), w_pair, grad_t)

    got = {step: turn(sent[step - 1], "slab", step) for step in (2, 1, 3)}
    weight_grad = (kept + got[2] + got[1] + got[3]).reshape(3, 3, mid // slabs, wide)
    gathered = lax.all_to_all(conv, "cout", 0, 0, tiled=True)
    output = jnp.sum(gathered, axis=0)
    return (output, weight_grad)


def solution(mesh):
    in_specs = (
        P("slab", None, "cin"),
        P(None, None, "cin", "cout"),
        P(None, None, "cout", "cin"),
        P("slab", None, "cin"),
    )
    out_specs = (P("slab", "cout", "cin"), P(None, None, ("cout", "slab"), "cin"))
    return jax.shard_map(
        block, mesh=mesh, in_specs=in_specs, out_specs=out_specs, check_vma=False
    )
```

```python
import functools

import jax
import jax.numpy as jnp
from jax import lax
from jax.experimental import pallas as pl
from jax.experimental.pallas import tpu as pltpu
from jax.sharding import Mesh, PartitionSpec as P


F32, BF16 = jnp.float32, jnp.bfloat16
VMEM = pl.BlockSpec(memory_space=pltpu.VMEM)
HBM = pl.BlockSpec(memory_space=pltpu.HBM)
SMEM = pl.BlockSpec(memory_space=pltpu.SMEM)
CORES = 2
LIMIT = pltpu.CompilerParams(vmem_limit_bytes=24 * 2**20)


def near(value):
    return pltpu.with_memory_space_constraint(value, pltpu.VMEM)


def far(value):
    return pltpu.with_memory_space_constraint(value, pltpu.HBM)


def shift(value, axis, step):
    count = lax.axis_size(axis)
    pairs = [(i, i + step) for i in range(count) if 0 <= i + step < count]
    return lax.ppermute(value, axis, pairs)


def trade(value, axis, step):
    count = lax.axis_size(axis)
    return lax.ppermute(value, axis, [(i, i ^ step) for i in range(count)])


def split(value):
    high = value.astype(BF16)
    return high, (value - high.astype(F32)).astype(BF16)


def dot(left, right):
    return jnp.dot(left, right, preferred_element_type=F32)


def taps_of_row(row):
    count = row.shape[0]
    at = lax.broadcasted_iota(jnp.int32, row.shape, 0)
    left = jnp.where(at == 0, 0.0, pltpu.roll(row, 1, 0))
    right = jnp.where(at == count - 1, 0.0, pltpu.roll(row, count - 1, 0))
    return left, row, right


def store_taps(row, high, low, start):
    rows, width = row.shape
    for tap, value in enumerate(taps_of_row(row)):
        top, rest = split(value)
        high[start : start + rows, tap * width : (tap + 1) * width] = top
        low[start : start + rows, tap * width : (tap + 1) * width] = rest


def first_prepare(image, weight, high, low, w_high, w_low, image_at, weight_at, sems):
    fetch_image = pltpu.make_async_copy(image, image_at, sems.at[0])
    fetch_weight = pltpu.make_async_copy(weight, weight_at, sems.at[1])
    fetch_image.start()
    fetch_weight.start()
    fetch_image.wait()
    rows, cols, depth = image_at.shape
    for row in range(rows):
        store_taps(image_at[row], high, low, row * cols)
    fetch_weight.wait()
    for tap in range(9):
        top, rest = split(weight_at[tap])
        w_high[tap // 3, (tap % 3) * depth : (tap % 3 + 1) * depth, :] = top
        w_low[tap // 3, (tap % 3) * depth : (tap % 3 + 1) * depth, :] = rest


def half_conv(out, part, cols, high, low, w_high, w_low):
    half = out.shape[0]
    total = None
    for a in range(3):
        rows = pl.ds(pl.multiple_of(part * half + a * cols, cols), half)
        term = dot(high[rows, :], w_high[a])
        term += dot(low[rows, :], w_high[a])
        term += dot(high[rows, :], w_low[a])
        total = term if total is None else total + term
    out[...] = total


def first_given(core, above, below, high_in, low_in, w_high, w_low, given, high, low):
    edge, cols, _ = above.shape
    inner = high_in.shape[0]
    high[edge * cols : edge * cols + inner, :] = high_in[...]
    low[edge * cols : edge * cols + inner, :] = low_in[...]
    for row in range(edge):
        store_taps(above[row], high, low, row * cols)
        store_taps(below[row], high, low, (edge + row) * cols + inner)
    half_conv(given, 1 - core[0], cols, high, low, w_high, w_low)


def first_held(cols, core, high, low, w_high, w_low, held):
    half_conv(held, core[0], cols, high, low, w_high, w_low)


def prepare(weight, grad, w_pair, grad_t):
    depth, wide = weight.shape[1], weight.shape[2]
    for tap in range(9):
        top, rest = split(weight[tap])
        w_pair[tap // 3, (tap % 3) * depth : (tap % 3 + 1) * depth, :wide] = top
        w_pair[tap // 3, (tap % 3) * depth : (tap % 3 + 1) * depth, wide:] = rest
    top, rest = split(grad[...].T)
    grad_t[:wide, :] = top
    grad_t[wide:, :] = rest


def activate(ends, pieces, own):
    total = pieces[0]
    for piece in range(1, pieces.shape[0]):
        total += pieces[piece]
    pixel = ends[0] + lax.broadcasted_iota(jnp.int32, total.shape, 0)
    inside = (pixel >= ends[1]) & (pixel < ends[2])
    own[...] = jnp.where(inside, total / (1.0 + jnp.exp(-total)), 0.0)


def second_conv(slab, hidden, w_pair, grad_t, conv, *rest):
    *local, ordered, high, low, turned = rest
    n_in, chunk, depth = hidden.shape
    chips = n_in // CORES
    n_out, rows, width, wide = conv.shape
    cols = n_out * width
    for core in range(CORES):
        for chip in range(chips):
            start = (core * chips + chip) * chunk
            ordered[start : start + chunk, :] = hidden[chip * CORES + core]
    for row in range(rows + 2):
        store_taps(ordered[row * cols : (row + 1) * cols, :], high, low, row * cols)
    slabs = len(local)
    part = local[0].shape[1]
    mine = slab[0]
    pixels = rows * cols
    for a in range(3):
        window = slice(a * cols, a * cols + pixels)
        for b in range(3):
            lanes = slice(b * depth, (b + 1) * depth)
            both = dot(grad_t[...], high[window, lanes])
            total = both[:wide] + both[wide:] + dot(grad_t[:wide, :], low[window, lanes])
            turned[...] = total.T
            for step in range(slabs):
                start = pl.multiple_of((mine ^ step) * part, part)
                local[step][a * 3 + b] = turned[pl.ds(start, part), :]
    main = None
    other = None
    for a in range(3):
        window = slice(a * cols, a * cols + pixels)
        one = dot(high[window, :], w_pair[a])
        two = dot(low[window, :], w_pair[a, :, :wide])
        main = one if main is None else main + one
        other = two if other is None else other + two
    total = main[:, :wide] + main[:, wide:] + other
    for row in range(rows):
        for block in range(n_out):
            start = row * cols + block * width
            conv[block, row] = total[start : start + width, :]


def block(image_in, first_weight, second_weight, out_grad):
    rows, cols, depth = image_in.shape
    mid = first_weight.shape[3]
    wide = second_weight.shape[3]
    slabs, chips, n_out = lax.axis_size("slab"), lax.axis_size("chip"), lax.axis_size("cout")
    slab, chip, core = lax.axis_index("slab"), lax.axis_index("chip"), lax.axis_index("core")
    ext = (rows + 2) * cols
    half = ext // CORES
    chunk = half // chips

    above = shift(image_in[rows - 2 :], "slab", 1)
    below = shift(image_in[:2], "slab", -1)
    weights = [pltpu.VMEM((3, 3 * depth, mid), BF16)] * 2
    inner = [pltpu.VMEM((rows * cols, 3 * depth), BF16)] * 2
    outer = [pltpu.VMEM(((rows + 4) * cols, 3 * depth), BF16)] * 2
    *image_parts, w_high, w_low = pl.pallas_call(
        first_prepare,
        out_shape=inner + weights,
        in_specs=[HBM] * 2,
        out_specs=[VMEM] * 4,
        scratch_shapes=[
            pltpu.VMEM((rows, cols, depth), F32),
            pltpu.VMEM((9, depth, mid), F32),
            pltpu.SemaphoreType.DMA((2,)),
        ],
        name="first_prepare",
        compiler_params=LIMIT,
    )(far(image_in), far(first_weight.reshape(9, depth, mid)))
    given, high, low = pl.pallas_call(
        first_given,
        out_shape=[pltpu.VMEM((half, mid), F32)] + outer,
        in_specs=[SMEM] + [VMEM] * 6,
        out_specs=[VMEM] * 3,
        name="first_given",
        compiler_params=LIMIT,
    )(core[None], *map(near, (above, below, *image_parts, w_high, w_low)))
    held = pl.pallas_call(
        functools.partial(first_held, cols),
        out_shape=pltpu.VMEM((half, mid), F32),
        in_specs=[SMEM] + [VMEM] * 4,
        out_specs=VMEM,
        name="first_held",
        compiler_params=LIMIT,
    )(core[None], *map(near, (high, low, w_high, w_low)))

    w_pair, grad_t = pl.pallas_call(
        prepare,
        out_shape=[
            pltpu.VMEM((3, 3 * mid, 2 * wide), BF16),
            pltpu.VMEM((2 * wide, rows * cols), BF16),
        ],
        in_specs=[VMEM] * 2,
        out_specs=[VMEM] * 2,
        name="prepare",
        compiler_params=LIMIT,
    )(second_weight.reshape(9, mid, wide), out_grad.reshape(rows * cols, wide))

    held = held + lax.ppermute(given, "core", [(0, 1), (1, 0)])
    pieces = lax.all_to_all(held.reshape(chips, chunk, mid), "chip", 0, 0, tiled=True)
    low_end = jnp.where(slab == 0, cols, 0)
    high_end = jnp.where(slab == slabs - 1, ext - cols, ext)
    own = pl.pallas_call(
        activate,
        out_shape=pltpu.VMEM((chunk, mid), F32),
        in_specs=[SMEM, VMEM],
        out_specs=VMEM,
        name="activate",
        compiler_params=LIMIT,
    )(jnp.stack([(core * chips + chip) * chunk, low_end, high_end]), near(pieces))
    hidden = lax.all_gather(own, ("chip", "core"), axis=0, tiled=False)

    conv, kept, *sent = pl.pallas_call(
        second_conv,
        out_shape=[pltpu.VMEM((n_out, rows, cols // n_out, wide), F32)]
        + [pltpu.VMEM((9, mid // slabs, wide), F32)] * slabs,
        in_specs=[SMEM] + [VMEM] * 3,
        out_specs=[VMEM] * (1 + slabs),
        scratch_shapes=[
            pltpu.VMEM((ext, mid), F32),
            pltpu.VMEM((ext, 3 * mid), BF16),
            pltpu.VMEM((ext, 3 * mid), BF16),
            pltpu.VMEM((mid, wide), F32),
        ],
        name="second_conv",
        compiler_params=LIMIT,
    )(slab[None], near(hidden), near(w_pair), near(grad_t))

    got = {step: trade(sent[step - 1], "slab", step) for step in (2, 1, 3)}
    weight_grad = (kept + got[2] + got[1] + got[3]).reshape(3, 3, mid // slabs, wide)
    gathered = lax.all_to_all(conv, "cout", 0, 0, tiled=True)
    output = jnp.sum(gathered, axis=0)
    return (output, weight_grad)


def solution(mesh):
    cin = ("chip", "core")
    in_specs = (
        P("slab", None, cin),
        P(None, None, cin, "cout"),
        P(None, None, "cout", cin),
        P("slab", None, cin),
    )
    out_specs = (P("slab", "cout", cin), P(None, None, ("cout", "slab"), cin))
    slabs, n_out, n_in = mesh.devices.shape
    devices = mesh.devices.reshape(slabs, n_out, n_in // CORES, CORES)
    split_mesh = Mesh(devices, ("slab", "cout", *cin))
    return jax.shard_map(
        block, mesh=split_mesh, in_specs=in_specs, out_specs=out_specs, check_vma=False
    )
```

```python
import functools

import jax
import jax.numpy as jnp
from jax import lax
from jax.experimental import pallas as pl
from jax.experimental.pallas import tpu as pltpu
from jax.sharding import Mesh, PartitionSpec as P


F32, BF16 = jnp.float32, jnp.bfloat16
VMEM = pl.BlockSpec(memory_space=pltpu.VMEM)
HBM = pl.BlockSpec(memory_space=pltpu.HBM)
SMEM = pl.BlockSpec(memory_space=pltpu.SMEM)
CORES = 2
LIMIT = pltpu.CompilerParams(vmem_limit_bytes=24 * 2**20)


def near(value):
    return pltpu.with_memory_space_constraint(value, pltpu.VMEM)


def far(value):
    return pltpu.with_memory_space_constraint(value, pltpu.HBM)


def shift(value, axis, step):
    count = lax.axis_size(axis)
    pairs = [(i, i + step) for i in range(count) if 0 <= i + step < count]
    return lax.ppermute(value, axis, pairs)


def trade(value, axis, step):
    count = lax.axis_size(axis)
    return lax.ppermute(value, axis, [(i, i ^ step) for i in range(count)])


def split(value):
    high = value.astype(BF16)
    return high, (value - high.astype(F32)).astype(BF16)


def dot(left, right):
    return jnp.dot(left, right, preferred_element_type=F32)


def taps_of_row(row):
    count = row.shape[0]
    at = lax.broadcasted_iota(jnp.int32, row.shape, 0)
    left = jnp.where(at == 0, 0.0, pltpu.roll(row, 1, 0))
    right = jnp.where(at == count - 1, 0.0, pltpu.roll(row, count - 1, 0))
    return left, row, right


def store_taps(row, high, low, start):
    rows, width = row.shape
    for tap, value in enumerate(taps_of_row(row)):
        top, rest = split(value)
        high[start : start + rows, tap * width : (tap + 1) * width] = top
        low[start : start + rows, tap * width : (tap + 1) * width] = rest


def first_prepare(image, weight, high, low, w_high, w_low, image_at, weight_at, sems):
    fetch_image = pltpu.make_async_copy(image, image_at, sems.at[0])
    fetch_weight = pltpu.make_async_copy(weight, weight_at, sems.at[1])
    fetch_image.start()
    fetch_weight.start()
    fetch_image.wait()
    rows, cols, depth = image_at.shape
    for row in range(rows):
        store_taps(image_at[row], high, low, row * cols)
    fetch_weight.wait()
    for tap in range(9):
        top, rest = split(weight_at[tap])
        w_high[tap // 3, (tap % 3) * depth : (tap % 3 + 1) * depth, :] = top
        w_low[tap // 3, (tap % 3) * depth : (tap % 3 + 1) * depth, :] = rest


def half_conv(out, part, cols, high, low, w_high, w_low):
    half = out.shape[0]
    total = None
    for a in range(3):
        rows = pl.ds(pl.multiple_of(part * half + a * cols, cols), half)
        term = dot(high[rows, :], w_high[a])
        term += dot(low[rows, :], w_high[a])
        term += dot(high[rows, :], w_low[a])
        total = term if total is None else total + term
    out[...] = total


def first_given(core, above, below, high_in, low_in, w_high, w_low, given, high, low):
    edge, cols, _ = above.shape
    inner = high_in.shape[0]
    high[edge * cols : edge * cols + inner, :] = high_in[...]
    low[edge * cols : edge * cols + inner, :] = low_in[...]
    for row in range(edge):
        store_taps(above[row], high, low, row * cols)
        store_taps(below[row], high, low, (edge + row) * cols + inner)
    half_conv(given, 1 - core[0], cols, high, low, w_high, w_low)


def first_held(cols, core, high, low, w_high, w_low, held):
    half_conv(held, core[0], cols, high, low, w_high, w_low)


def prepare(weight, w_pair):
    depth, wide = weight.shape[1], weight.shape[2]
    for tap in range(9):
        top, rest = split(weight[tap])
        w_pair[tap // 3, (tap % 3) * depth : (tap % 3 + 1) * depth, :wide] = top
        w_pair[tap // 3, (tap % 3) * depth : (tap % 3 + 1) * depth, wide:] = rest


def turn_grads(slab, *refs):
    *grads, grad_t = refs
    wide = grads[0].shape[1]
    for step, grad in enumerate(grads):
        top, rest = split(grad[...].T)
        grad_t[slab[0] ^ step, :wide, :] = top
        grad_t[slab[0] ^ step, wide:, :] = rest


def activate(ends, pieces, own):
    total = pieces[0]
    for piece in range(1, pieces.shape[0]):
        total += pieces[piece]
    pixel = ends[0] + lax.broadcasted_iota(jnp.int32, total.shape, 0)
    inside = (pixel >= ends[1]) & (pixel < ends[2])
    own[...] = jnp.where(inside, total / (1.0 + jnp.exp(-total)), 0.0)


def lower_lanes(shape):
    return lax.broadcasted_iota(jnp.int32, shape, 1) < shape[1] // 2


def swap_lanes(value):
    return pltpu.roll(value, value.shape[1] // 2, 1)


def second_conv(slab, hidden, w_pair, conv, *rest):
    *local, ordered, high, low, packed = rest
    n_in, chunk, _ = hidden.shape
    chips = n_in // CORES
    n_out, rows, width, wide = conv.shape
    cols = n_out * width
    for core in range(CORES):
        for chip in range(chips):
            start = (core * chips + chip) * chunk
            ordered[start : start + chunk, :] = hidden[chip * CORES + core]
    count, lanes = local[0].shape
    for quarter in range(len(local)):
        at = slice(quarter // 2 * lanes, (quarter // 2 + 1) * lanes)
        first = ordered[cols : cols + count, at]
        second = ordered[cols + count : cols + 2 * count, at]
        if quarter % 2:
            first = swap_lanes(first)
        else:
            second = swap_lanes(second)
        packed[quarter] = jnp.where(lower_lanes(first.shape), first, second)
    for step, out in enumerate(local):
        out[...] = packed[slab[0] ^ step]
    for row in range(rows + 2):
        store_taps(ordered[row * cols : (row + 1) * cols, :], high, low, row * cols)
    pixels = rows * cols
    main = None
    other = None
    for a in range(3):
        window = slice(a * cols, a * cols + pixels)
        one = dot(high[window, :], w_pair[a])
        two = dot(low[window, :], w_pair[a, :, :wide])
        main = one if main is None else main + one
        other = two if other is None else other + two
    total = main[:, :wide] + main[:, wide:] + other
    for row in range(rows):
        for block in range(n_out):
            start = row * cols + block * width
            conv[block, row] = total[start : start + width, :]


def weight_sums(cols, slab, *refs):
    *local, grad_t, out, high, low = refs
    slabs = len(local)
    count, lanes = local[0].shape
    part = lanes // 2
    wide = out.shape[2]
    blank = jnp.zeros((cols, 2 * lanes), BF16)
    end = high.shape[0] - cols
    for ref in (high, low):
        ref[0:cols, :] = blank
        ref[end : end + cols, :] = blank
    for step, source in enumerate(local):
        base = cols + (slab[0] ^ step) * 2 * count
        for row in range(count // cols):
            left, here, right = taps_of_row(source[row * cols : (row + 1) * cols, :])
            lower = lower_lanes(here.shape)
            pairs = (
                (jnp.where(lower, left, swap_lanes(here)), right),
                (jnp.where(lower, swap_lanes(left), here), swap_lanes(right)),
            )
            for half, pair in enumerate(pairs):
                start = pl.multiple_of(base + half * count + row * cols, cols)
                for k, value in enumerate(pair):
                    top, rest = split(value)
                    high[pl.ds(start, cols), k * lanes : (k + 1) * lanes] = top
                    low[pl.ds(start, cols), k * lanes : (k + 1) * lanes] = rest
    for a in range(3):
        main = None
        other = None
        for j in range(slabs):
            window = slice(a * cols + j * 2 * count, a * cols + (j + 1) * 2 * count)
            one = dot(grad_t[j], high[window, :])
            two = dot(grad_t[j, :wide, :], low[window, :])
            main = one if main is None else main + one
            other = two if other is None else other + two
        turned = (main[:wide] + main[wide:] + other).T
        for b in range(3):
            out[a * 3 + b] = turned[b * part : (b + 1) * part, :]


def block(image_in, first_weight, second_weight, out_grad):
    rows, cols, depth = image_in.shape
    mid = first_weight.shape[3]
    wide = second_weight.shape[3]
    slabs, chips, n_out = lax.axis_size("slab"), lax.axis_size("chip"), lax.axis_size("cout")
    slab, chip, core = lax.axis_index("slab"), lax.axis_index("chip"), lax.axis_index("core")
    ext = (rows + 2) * cols
    half = ext // CORES
    chunk = half // chips

    above = shift(image_in[rows - 2 :], "slab", 1)
    below = shift(image_in[:2], "slab", -1)
    weights = [pltpu.VMEM((3, 3 * depth, mid), BF16)] * 2
    inner = [pltpu.VMEM((rows * cols, 3 * depth), BF16)] * 2
    outer = [pltpu.VMEM(((rows + 4) * cols, 3 * depth), BF16)] * 2
    *image_parts, w_high, w_low = pl.pallas_call(
        first_prepare,
        out_shape=inner + weights,
        in_specs=[HBM] * 2,
        out_specs=[VMEM] * 4,
        scratch_shapes=[
            pltpu.VMEM((rows, cols, depth), F32),
            pltpu.VMEM((9, depth, mid), F32),
            pltpu.SemaphoreType.DMA((2,)),
        ],
        name="first_prepare",
        compiler_params=LIMIT,
    )(far(image_in), far(first_weight.reshape(9, depth, mid)))
    given, high, low = pl.pallas_call(
        first_given,
        out_shape=[pltpu.VMEM((half, mid), F32)] + outer,
        in_specs=[SMEM] + [VMEM] * 6,
        out_specs=[VMEM] * 3,
        name="first_given",
        compiler_params=LIMIT,
    )(core[None], *map(near, (above, below, *image_parts, w_high, w_low)))
    held = pl.pallas_call(
        functools.partial(first_held, cols),
        out_shape=pltpu.VMEM((half, mid), F32),
        in_specs=[SMEM] + [VMEM] * 4,
        out_specs=VMEM,
        name="first_held",
        compiler_params=LIMIT,
    )(core[None], *map(near, (high, low, w_high, w_low)))

    w_pair = pl.pallas_call(
        prepare,
        out_shape=pltpu.VMEM((3, 3 * mid, 2 * wide), BF16),
        in_specs=[VMEM],
        out_specs=VMEM,
        name="prepare",
        compiler_params=LIMIT,
    )(second_weight.reshape(9, mid, wide))

    held = held + lax.ppermute(given, "core", [(0, 1), (1, 0)])
    pieces = lax.all_to_all(held.reshape(chips, chunk, mid), "chip", 0, 0, tiled=True)
    grads = [out_grad.reshape(rows * cols, wide)]
    grads += [trade(grads[0], "slab", step) for step in range(1, slabs)]
    low_end = jnp.where(slab == 0, cols, 0)
    high_end = jnp.where(slab == slabs - 1, ext - cols, ext)
    own = pl.pallas_call(
        activate,
        out_shape=pltpu.VMEM((chunk, mid), F32),
        in_specs=[SMEM, VMEM],
        out_specs=VMEM,
        name="activate",
        compiler_params=LIMIT,
    )(jnp.stack([(core * chips + chip) * chunk, low_end, high_end]), near(pieces))
    hidden = lax.all_gather(own, ("chip", "core"), axis=0, tiled=False)

    lanes = 2 * mid // slabs
    count = rows * cols // 2
    conv, *local = pl.pallas_call(
        second_conv,
        out_shape=[pltpu.VMEM((n_out, rows, cols // n_out, wide), F32)]
        + [pltpu.VMEM((count, lanes), F32)] * slabs,
        in_specs=[SMEM] + [VMEM] * 2,
        out_specs=[VMEM] * (1 + slabs),
        scratch_shapes=[
            pltpu.VMEM((ext, mid), F32),
            pltpu.VMEM((ext, 3 * mid), BF16),
            pltpu.VMEM((ext, 3 * mid), BF16),
            pltpu.VMEM((slabs, count, lanes), F32),
        ],
        name="second_conv",
        compiler_params=LIMIT,
    )(slab[None], near(hidden), near(w_pair))

    gathered = lax.all_to_all(conv, "cout", 0, 0, tiled=True)
    local[1:] = [trade(local[step], "slab", step) for step in range(1, slabs)]
    grad_t = pl.pallas_call(
        turn_grads,
        out_shape=pltpu.VMEM((slabs, 2 * wide, rows * cols), BF16),
        in_specs=[SMEM] + [VMEM] * slabs,
        out_specs=VMEM,
        name="turn_grads",
        compiler_params=LIMIT,
    )(slab[None], *map(near, grads))
    weight_grad = pl.pallas_call(
        functools.partial(weight_sums, cols),
        out_shape=jax.ShapeDtypeStruct((9, mid // slabs, wide), F32),
        in_specs=[SMEM] + [VMEM] * (slabs + 1),
        out_specs=VMEM,
        scratch_shapes=[
            pltpu.VMEM(((slabs * rows + 2) * cols, 2 * lanes), BF16),
            pltpu.VMEM(((slabs * rows + 2) * cols, 2 * lanes), BF16),
        ],
        name="weight_sums",
        compiler_params=LIMIT,
    )(slab[None], *map(near, local), near(grad_t))
    weight_grad = weight_grad.reshape(3, 3, mid // slabs, wide)
    output = jnp.sum(gathered, axis=0)
    return (output, weight_grad)


def solution(mesh):
    cin = ("chip", "core")
    in_specs = (
        P("slab", None, cin),
        P(None, None, cin, "cout"),
        P(None, None, "cout", cin),
        P("slab", None, cin),
    )
    out_specs = (P("slab", "cout", cin), P(None, None, ("cout", "slab"), cin))
    slabs, n_out, n_in = mesh.devices.shape
    devices = mesh.devices.reshape(slabs, n_out, n_in // CORES, CORES)
    split_mesh = Mesh(devices, ("slab", "cout", *cin))
    return jax.shard_map(
        block, mesh=split_mesh, in_specs=in_specs, out_specs=out_specs, check_vma=False
    )
```

```python
import functools

import jax
import jax.numpy as jnp
from jax import lax
from jax.experimental import pallas as pl
from jax.experimental.pallas import tpu as pltpu
from jax.sharding import Mesh, PartitionSpec as P


F32, BF16 = jnp.float32, jnp.bfloat16
VMEM = pl.BlockSpec(memory_space=pltpu.VMEM)
HBM = pl.BlockSpec(memory_space=pltpu.HBM)
SMEM = pl.BlockSpec(memory_space=pltpu.SMEM)
CORES = 2
STEPS = (0, 2, 1, 3)
LIMIT = pltpu.CompilerParams(vmem_limit_bytes=24 * 2**20)


def near(value):
    return pltpu.with_memory_space_constraint(value, pltpu.VMEM)


def far(value):
    return pltpu.with_memory_space_constraint(value, pltpu.HBM)


def shift(value, axis, step):
    count = lax.axis_size(axis)
    pairs = [(i, i + step) for i in range(count) if 0 <= i + step < count]
    return lax.ppermute(value, axis, pairs)


def trade(value, axis, step):
    count = lax.axis_size(axis)
    return lax.ppermute(value, axis, [(i, i ^ step) for i in range(count)])


def split(value):
    high = value.astype(BF16)
    return high, (value - high.astype(F32)).astype(BF16)


def dot(left, right):
    return jnp.dot(left, right, preferred_element_type=F32)


def taps_of_row(row):
    count = row.shape[0]
    at = lax.broadcasted_iota(jnp.int32, row.shape, 0)
    left = jnp.where(at == 0, 0.0, pltpu.roll(row, 1, 0))
    right = jnp.where(at == count - 1, 0.0, pltpu.roll(row, count - 1, 0))
    return left, row, right


def store_taps(row, high, low, start):
    rows, width = row.shape
    for tap, value in enumerate(taps_of_row(row)):
        top, rest = split(value)
        high[start : start + rows, tap * width : (tap + 1) * width] = top
        low[start : start + rows, tap * width : (tap + 1) * width] = rest


def first_prepare(image, weight, high, low, w_high, w_low, image_at, weight_at, sems):
    fetch_image = pltpu.make_async_copy(image, image_at, sems.at[0])
    fetch_weight = pltpu.make_async_copy(weight, weight_at, sems.at[1])
    fetch_image.start()
    fetch_weight.start()
    fetch_image.wait()
    rows, cols, depth = image_at.shape
    for row in range(rows):
        store_taps(image_at[row], high, low, row * cols)
    fetch_weight.wait()
    for tap in range(9):
        top, rest = split(weight_at[tap])
        w_high[tap // 3, (tap % 3) * depth : (tap % 3 + 1) * depth, :] = top
        w_low[tap // 3, (tap % 3) * depth : (tap % 3 + 1) * depth, :] = rest


def half_conv(out, part, cols, high, low, w_high, w_low):
    half = out.shape[0]
    total = None
    for a in range(3):
        rows = pl.ds(pl.multiple_of(part * half + a * cols, cols), half)
        term = dot(high[rows, :], w_high[a])
        term += dot(low[rows, :], w_high[a])
        term += dot(high[rows, :], w_low[a])
        total = term if total is None else total + term
    out[...] = total


def first_given(core, above, below, high_in, low_in, w_high, w_low, given, high, low):
    edge, cols, _ = above.shape
    inner = high_in.shape[0]
    high[edge * cols : edge * cols + inner, :] = high_in[...]
    low[edge * cols : edge * cols + inner, :] = low_in[...]
    for row in range(edge):
        store_taps(above[row], high, low, row * cols)
        store_taps(below[row], high, low, (edge + row) * cols + inner)
    half_conv(given, 1 - core[0], cols, high, low, w_high, w_low)


def first_held(cols, core, high, low, w_high, w_low, held):
    half_conv(held, core[0], cols, high, low, w_high, w_low)


def prepare(weight, w_pair):
    depth, wide = weight.shape[1], weight.shape[2]
    for tap in range(9):
        top, rest = split(weight[tap])
        w_pair[tap // 3, (tap % 3) * depth : (tap % 3 + 1) * depth, :wide] = top
        w_pair[tap // 3, (tap % 3) * depth : (tap % 3 + 1) * depth, wide:] = rest


def activate(ends, pieces, own):
    total = pieces[0]
    for piece in range(1, pieces.shape[0]):
        total += pieces[piece]
    pixel = ends[0] + lax.broadcasted_iota(jnp.int32, total.shape, 0)
    inside = (pixel >= ends[1]) & (pixel < ends[2])
    own[...] = jnp.where(inside, total / (1.0 + jnp.exp(-total)), 0.0)


def lower_lanes(shape):
    return lax.broadcasted_iota(jnp.int32, shape, 1) < shape[1] // 2


def swap_lanes(value):
    return pltpu.roll(value, value.shape[1] // 2, 1)


def second_conv(slab, hidden, w_pair, conv, *rest):
    *local, ordered, high, low, packed = rest
    n_in, chunk, _ = hidden.shape
    chips = n_in // CORES
    n_out, rows, width, wide = conv.shape
    cols = n_out * width
    for core in range(CORES):
        for chip in range(chips):
            start = (core * chips + chip) * chunk
            ordered[start : start + chunk, :] = hidden[chip * CORES + core]
    count, lanes = local[0].shape
    for quarter in range(len(local)):
        at = slice(quarter // 2 * lanes, (quarter // 2 + 1) * lanes)
        first = ordered[cols : cols + count, at]
        second = ordered[cols + count : cols + 2 * count, at]
        if quarter % 2:
            first = swap_lanes(first)
        else:
            second = swap_lanes(second)
        packed[quarter] = jnp.where(lower_lanes(first.shape), first, second)
    for step, out in zip(STEPS, local, strict=True):
        out[...] = packed[slab[0] ^ step]
    for row in range(rows + 2):
        store_taps(ordered[row * cols : (row + 1) * cols, :], high, low, row * cols)
    pixels = rows * cols
    main = None
    other = None
    for a in range(3):
        window = slice(a * cols, a * cols + pixels)
        one = dot(high[window, :], w_pair[a])
        two = dot(low[window, :], w_pair[a, :, :wide])
        main = one if main is None else main + one
        other = two if other is None else other + two
    total = main[:, :wide] + main[:, wide:] + other
    for row in range(rows):
        for block in range(n_out):
            start = row * cols + block * width
            conv[block, row] = total[start : start + width, :]


def pixel_sums(cols, source, grad_t, high, low):
    count, lanes = source.shape
    wide = grad_t.shape[1] // 2
    for row in range(count // cols):
        left, here, right = taps_of_row(source[row * cols : (row + 1) * cols, :])
        lower = lower_lanes(here.shape)
        pairs = (
            (jnp.where(lower, left, swap_lanes(here)), right),
            (jnp.where(lower, swap_lanes(left), here), swap_lanes(right)),
        )
        for half, pair in enumerate(pairs):
            at = slice(half * count + row * cols, half * count + (row + 1) * cols)
            for k, value in enumerate(pair):
                top, rest = split(value)
                high[at, k * lanes : (k + 1) * lanes] = top
                low[at, k * lanes : (k + 1) * lanes] = rest
    sums = []
    for a in range(3):
        both = dot(grad_t[a], high[...])
        sums.append(both[:wide] + both[wide:] + dot(grad_t[a, :wide, :], low[...]))
    return sums


def early_sums(cols, slab, *refs):
    *refs, out, grad_last, high, low, grad_t, whole, sems = refs
    slabs = sems.shape[0]
    grads, local = refs[:slabs], refs[slabs:]
    pixels, wide = grads[0].shape
    early = len(local)
    copies = []
    for step, grad in enumerate(grads):
        start = pl.multiple_of(cols + (slab[0] ^ STEPS[step]) * pixels, cols)
        copies.append(
            pltpu.make_async_copy(grad, whole.at[pl.ds(start, pixels), :], sems.at[step])
        )
        copies[step].start()
    blank = jnp.zeros((cols, wide), F32)
    end = whole.shape[0] - cols
    whole[0:cols, :] = blank
    whole[end : end + cols, :] = blank
    for copy in copies:
        copy.wait()
    for step in range(slabs):
        into = grad_t.at[step] if step < early else grad_last.at[step - early]
        for a in range(3):
            start = pl.multiple_of((2 - a) * cols + (slab[0] ^ STEPS[step]) * pixels, cols)
            top, rest = split(whole[pl.ds(start, pixels), :].T)
            into[a, :wide, :] = top
            into[a, wide:, :] = rest
    for step, source in enumerate(local):
        for a, value in enumerate(pixel_sums(cols, source, grad_t.at[step], high, low)):
            out[a] = value if step == 0 else out[a] + value


def last_sums(cols, *refs):
    *local, grad_t, sums, after, out, high, low = refs
    part = out.shape[1]
    terms = [
        pixel_sums(cols, source, grad_t.at[step], high, low) for step, source in enumerate(local)
    ]
    for a in range(3):
        turned = sum((term[a] for term in terms), sums[a]).T
        for b in range(3):
            out[a * 3 + b] = turned[b * part : (b + 1) * part, :]


def block(image_in, first_weight, second_weight, out_grad):
    rows, cols, depth = image_in.shape
    mid = first_weight.shape[3]
    wide = second_weight.shape[3]
    slabs, chips, n_out = lax.axis_size("slab"), lax.axis_size("chip"), lax.axis_size("cout")
    slab, chip, core = lax.axis_index("slab"), lax.axis_index("chip"), lax.axis_index("core")
    ext = (rows + 2) * cols
    half = ext // CORES
    chunk = half // chips

    above = shift(image_in[rows - 2 :], "slab", 1)
    below = shift(image_in[:2], "slab", -1)
    weights = [pltpu.VMEM((3, 3 * depth, mid), BF16)] * 2
    inner = [pltpu.VMEM((rows * cols, 3 * depth), BF16)] * 2
    outer = [pltpu.VMEM(((rows + 4) * cols, 3 * depth), BF16)] * 2
    *image_parts, w_high, w_low = pl.pallas_call(
        first_prepare,
        out_shape=inner + weights,
        in_specs=[HBM] * 2,
        out_specs=[VMEM] * 4,
        scratch_shapes=[
            pltpu.VMEM((rows, cols, depth), F32),
            pltpu.VMEM((9, depth, mid), F32),
            pltpu.SemaphoreType.DMA((2,)),
        ],
        name="first_prepare",
        compiler_params=LIMIT,
    )(far(image_in), far(first_weight.reshape(9, depth, mid)))
    given, high, low = pl.pallas_call(
        first_given,
        out_shape=[pltpu.VMEM((half, mid), F32)] + outer,
        in_specs=[SMEM] + [VMEM] * 6,
        out_specs=[VMEM] * 3,
        name="first_given",
        compiler_params=LIMIT,
    )(core[None], *map(near, (above, below, *image_parts, w_high, w_low)))
    held = pl.pallas_call(
        functools.partial(first_held, cols),
        out_shape=pltpu.VMEM((half, mid), F32),
        in_specs=[SMEM] + [VMEM] * 4,
        out_specs=VMEM,
        name="first_held",
        compiler_params=LIMIT,
    )(core[None], *map(near, (high, low, w_high, w_low)))

    w_pair = pl.pallas_call(
        prepare,
        out_shape=pltpu.VMEM((3, 3 * mid, 2 * wide), BF16),
        in_specs=[VMEM],
        out_specs=VMEM,
        name="prepare",
        compiler_params=LIMIT,
    )(second_weight.reshape(9, mid, wide))

    held = held + lax.ppermute(given, "core", [(0, 1), (1, 0)])
    pieces = lax.all_to_all(held.reshape(chips, chunk, mid), "chip", 0, 0, tiled=True)
    grads = [out_grad.reshape(rows * cols, wide)]
    grads += [trade(grads[0], "slab", step) for step in STEPS[1:]]
    low_end = jnp.where(slab == 0, cols, 0)
    high_end = jnp.where(slab == slabs - 1, ext - cols, ext)
    own = pl.pallas_call(
        activate,
        out_shape=pltpu.VMEM((chunk, mid), F32),
        in_specs=[SMEM, VMEM],
        out_specs=VMEM,
        name="activate",
        compiler_params=LIMIT,
    )(jnp.stack([(core * chips + chip) * chunk, low_end, high_end]), near(pieces))
    hidden = lax.all_gather(own, ("chip", "core"), axis=0, tiled=False)

    lanes = 2 * mid // slabs
    count = rows * cols // 2
    conv, *local = pl.pallas_call(
        second_conv,
        out_shape=[pltpu.VMEM((n_out, rows, cols // n_out, wide), F32)]
        + [pltpu.VMEM((count, lanes), F32)] * slabs,
        in_specs=[SMEM] + [VMEM] * 2,
        out_specs=[VMEM] * (1 + slabs),
        scratch_shapes=[
            pltpu.VMEM((ext, mid), F32),
            pltpu.VMEM((ext, 3 * mid), BF16),
            pltpu.VMEM((ext, 3 * mid), BF16),
            pltpu.VMEM((slabs, count, lanes), F32),
        ],
        name="second_conv",
        compiler_params=LIMIT,
    )(slab[None], near(hidden), near(w_pair))

    gathered = lax.all_to_all(conv, "cout", 0, 0, tiled=True)
    local[1:] = [trade(local[k], "slab", STEPS[k]) for k in range(1, slabs)]
    output = jnp.sum(gathered, axis=0)
    pixels = rows * cols
    early = slabs // 2
    tap_pair = [pltpu.VMEM((pixels, 2 * lanes), BF16)] * 2
    sums, grad_last = pl.pallas_call(
        functools.partial(early_sums, cols),
        out_shape=[
            pltpu.VMEM((3, wide, 2 * lanes), F32),
            pltpu.VMEM((slabs - early, 3, 2 * wide, pixels), BF16),
        ],
        in_specs=[SMEM] + [HBM] * slabs + [VMEM] * early,
        out_specs=[VMEM] * 2,
        scratch_shapes=tap_pair
        + [
            pltpu.VMEM((early, 3, 2 * wide, pixels), BF16),
            pltpu.VMEM((slabs * pixels + 2 * cols, wide), F32),
            pltpu.SemaphoreType.DMA((slabs,)),
        ],
        name="early_sums",
        compiler_params=LIMIT,
    )(slab[None], *map(far, grads), *map(near, local[:early]))
    weight_grad = pl.pallas_call(
        functools.partial(last_sums, cols),
        out_shape=jax.ShapeDtypeStruct((9, mid // slabs, wide), F32),
        in_specs=[VMEM] * (slabs - early + 2) + [HBM],
        out_specs=VMEM,
        scratch_shapes=tap_pair,
        name="last_sums",
        compiler_params=LIMIT,
    )(*map(near, (*local[early:], grad_last, sums)), far(output))
    weight_grad = weight_grad.reshape(3, 3, mid // slabs, wide)
    return (output, weight_grad)


def solution(mesh):
    cin = ("chip", "core")
    in_specs = (
        P("slab", None, cin),
        P(None, None, cin, "cout"),
        P(None, None, "cout", cin),
        P("slab", None, cin),
    )
    out_specs = (P("slab", "cout", cin), P(None, None, ("cout", "slab"), cin))
    slabs, n_out, n_in = mesh.devices.shape
    devices = mesh.devices.reshape(slabs, n_out, n_in // CORES, CORES)
    split_mesh = Mesh(devices, ("slab", "cout", *cin))
    return jax.shard_map(
        block, mesh=split_mesh, in_specs=in_specs, out_specs=out_specs, check_vma=False
    )
```

```python
import functools

import jax
import jax.numpy as jnp
from jax import lax
from jax.experimental import pallas as pl
from jax.experimental.pallas import tpu as pltpu
from jax.sharding import Mesh, PartitionSpec as P


F32, BF16 = jnp.float32, jnp.bfloat16
VMEM = pl.BlockSpec(memory_space=pltpu.VMEM)
HBM = pl.BlockSpec(memory_space=pltpu.HBM)
SMEM = pl.BlockSpec(memory_space=pltpu.SMEM)
CORES = 2
STEPS = (0, 2, 1, 3)
LIMIT = pltpu.CompilerParams(vmem_limit_bytes=24 * 2**20)


def near(value):
    return pltpu.with_memory_space_constraint(value, pltpu.VMEM)


def far(value):
    return pltpu.with_memory_space_constraint(value, pltpu.HBM)


def shift(value, axis, step):
    count = lax.axis_size(axis)
    pairs = [(i, i + step) for i in range(count) if 0 <= i + step < count]
    return lax.ppermute(value, axis, pairs)


def trade(value, axis, step):
    count = lax.axis_size(axis)
    return lax.ppermute(value, axis, [(i, i ^ step) for i in range(count)])


def split(value):
    high = value.astype(BF16)
    return high, (value - high.astype(F32)).astype(BF16)


def dot(left, right):
    return jnp.dot(left, right, preferred_element_type=F32)


def taps_of_row(row):
    count = row.shape[0]
    at = lax.broadcasted_iota(jnp.int32, row.shape, 0)
    left = jnp.where(at == 0, 0.0, pltpu.roll(row, 1, 0))
    right = jnp.where(at == count - 1, 0.0, pltpu.roll(row, count - 1, 0))
    return left, row, right


def store_taps(row, high, low, start):
    rows, width = row.shape
    for tap, value in enumerate(taps_of_row(row)):
        top, rest = split(value)
        high[start : start + rows, tap * width : (tap + 1) * width] = top
        low[start : start + rows, tap * width : (tap + 1) * width] = rest


def first_prepare(image, weight, high, low, w_high, w_low, image_at, weight_at, sems):
    fetch_image = pltpu.make_async_copy(image, image_at, sems.at[0])
    fetch_weight = pltpu.make_async_copy(weight, weight_at, sems.at[1])
    fetch_image.start()
    fetch_weight.start()
    fetch_image.wait()
    rows, cols, depth = image_at.shape
    for row in range(rows):
        store_taps(image_at[row], high, low, row * cols)
    fetch_weight.wait()
    for tap in range(9):
        top, rest = split(weight_at[tap])
        w_high[tap // 3, (tap % 3) * depth : (tap % 3 + 1) * depth, :] = top
        w_low[tap // 3, (tap % 3) * depth : (tap % 3 + 1) * depth, :] = rest


def half_conv(out, part, cols, high, low, w_high, w_low):
    half = out.shape[0]
    total = None
    for a in range(3):
        rows = pl.ds(pl.multiple_of(part * half + a * cols, cols), half)
        term = dot(high[rows, :], w_high[a])
        term += dot(low[rows, :], w_high[a])
        term += dot(high[rows, :], w_low[a])
        total = term if total is None else total + term
    out[...] = total


def first_given(core, above, below, high_in, low_in, w_high, w_low, given, high, low):
    edge, cols, _ = above.shape
    inner = high_in.shape[0]
    high[edge * cols : edge * cols + inner, :] = high_in[...]
    low[edge * cols : edge * cols + inner, :] = low_in[...]
    for row in range(edge):
        store_taps(above[row], high, low, row * cols)
        store_taps(below[row], high, low, (edge + row) * cols + inner)
    half_conv(given, 1 - core[0], cols, high, low, w_high, w_low)


def first_held(cols, core, high, low, w_high, w_low, held):
    half_conv(held, core[0], cols, high, low, w_high, w_low)


def prepare(weight, w_pair):
    depth, wide = weight.shape[1], weight.shape[2]
    for tap in range(9):
        top, rest = split(weight[tap])
        w_pair[tap // 3, (tap % 3) * depth : (tap % 3 + 1) * depth, :wide] = top
        w_pair[tap // 3, (tap % 3) * depth : (tap % 3 + 1) * depth, wide:] = rest


def activate(ends, pieces, own):
    total = pieces[0]
    for piece in range(1, pieces.shape[0]):
        total += pieces[piece]
    pixel = ends[0] + lax.broadcasted_iota(jnp.int32, total.shape, 0)
    inside = (pixel >= ends[1]) & (pixel < ends[2])
    own[...] = jnp.where(inside, total / (1.0 + jnp.exp(-total)), 0.0)


def lower_lanes(shape):
    return lax.broadcasted_iota(jnp.int32, shape, 1) < shape[1] // 2


def swap_lanes(value):
    return pltpu.roll(value, value.shape[1] // 2, 1)


def second_conv(slab, hidden, w_pair, conv, *rest):
    *local, ordered, high, low, packed = rest
    n_in, chunk, _ = hidden.shape
    chips = n_in // CORES
    n_out, rows, width, wide = conv.shape
    cols = n_out * width
    for core in range(CORES):
        for chip in range(chips):
            start = (core * chips + chip) * chunk
            ordered[start : start + chunk, :] = hidden[chip * CORES + core]
    count, lanes = local[0].shape
    for quarter in range(len(local)):
        at = slice(quarter // 2 * lanes, (quarter // 2 + 1) * lanes)
        first = ordered[cols : cols + count, at]
        second = ordered[cols + count : cols + 2 * count, at]
        if quarter % 2:
            first = swap_lanes(first)
        else:
            second = swap_lanes(second)
        packed[quarter] = jnp.where(lower_lanes(first.shape), first, second)
    for step, out in zip(STEPS, local, strict=True):
        out[...] = packed[slab[0] ^ step]
    for row in range(rows + 2):
        store_taps(ordered[row * cols : (row + 1) * cols, :], high, low, row * cols)
    pixels = rows * cols
    main = None
    other = None
    for a in range(3):
        window = slice(a * cols, a * cols + pixels)
        one = dot(high[window, :], w_pair[a])
        two = dot(low[window, :], w_pair[a, :, :wide])
        main = one if main is None else main + one
        other = two if other is None else other + two
    total = main[:, :wide] + main[:, wide:] + other
    for row in range(rows):
        for block in range(n_out):
            start = row * cols + block * width
            conv[block, row] = total[start : start + width, :]


def pixel_taps(cols, source, high, low):
    count, lanes = source.shape
    for row in range(count // cols):
        left, here, right = taps_of_row(source[row * cols : (row + 1) * cols, :])
        lower = lower_lanes(here.shape)
        pairs = (
            (jnp.where(lower, left, swap_lanes(here)), right),
            (jnp.where(lower, swap_lanes(left), here), swap_lanes(right)),
        )
        for half, pair in enumerate(pairs):
            at = slice(half * count + row * cols, half * count + (row + 1) * cols)
            for k, value in enumerate(pair):
                top, rest = split(value)
                high[at, k * lanes : (k + 1) * lanes] = top
                low[at, k * lanes : (k + 1) * lanes] = rest


def pixel_sums(grad_t, high, low):
    wide = grad_t.shape[1] // 2
    sums = []
    for a in range(3):
        both = dot(grad_t[a], high[...])
        sums.append(both[:wide] + both[wide:] + dot(grad_t[a, :wide, :], low[...]))
    return sums


def early_sums(cols, slab, *refs):
    *refs, out, grad_last, high, low, grad_t, whole, sems = refs
    slabs = sems.shape[0]
    grads, local = refs[:slabs], refs[slabs:]
    rows, _, wide = grads[0].shape
    early = len(local)
    copies = []
    for step, grad in enumerate(grads):
        into = whole.at[pl.ds(1 + (slab[0] ^ STEPS[step]) * rows, rows)]
        copies.append(pltpu.make_async_copy(grad, into, sems.at[step]))
        copies[step].start()
    blank = jnp.zeros((cols, wide), F32)
    whole[0] = blank
    whole[whole.shape[0] - 1] = blank
    for step, source in enumerate(local):
        pixel_taps(cols, source, high.at[step], low.at[step])
    for copy in copies:
        copy.wait()
    for step in range(slabs):
        into = grad_t.at[step] if step < early else grad_last.at[step - early]
        for a in range(3):
            window = whole[pl.ds((slab[0] ^ STEPS[step]) * rows + 2 - a, rows)]
            top, rest = split(window.reshape(rows * cols, wide).T)
            into[a, :wide, :] = top
            into[a, wide:, :] = rest
    for step in range(early):
        sums = pixel_sums(grad_t.at[step], high.at[step], low.at[step])
        for a, value in enumerate(sums):
            out[a] = value if step == 0 else out[a] + value


def last_sums(cols, *refs):
    *local, grad_t, sums, gathered, out, output, high, low = refs
    part = out.shape[1]
    terms = []
    for step, source in enumerate(local):
        pixel_taps(cols, source, high.at[step], low.at[step])
        terms.append(pixel_sums(grad_t.at[step], high.at[step], low.at[step]))
    for a in range(3):
        turned = sum((term[a] for term in terms), sums[a]).T
        for b in range(3):
            out[a * 3 + b] = turned[b * part : (b + 1) * part, :]
    total = gathered[0]
    for piece in range(1, gathered.shape[0]):
        total += gathered[piece]
    output[...] = total


def block(image_in, first_weight, second_weight, out_grad):
    rows, cols, depth = image_in.shape
    mid = first_weight.shape[3]
    wide = second_weight.shape[3]
    slabs, chips, n_out = lax.axis_size("slab"), lax.axis_size("chip"), lax.axis_size("cout")
    slab, chip, core = lax.axis_index("slab"), lax.axis_index("chip"), lax.axis_index("core")
    ext = (rows + 2) * cols
    half = ext // CORES
    chunk = half // chips

    above = shift(image_in[rows - 2 :], "slab", 1)
    below = shift(image_in[:2], "slab", -1)
    weights = [pltpu.VMEM((3, 3 * depth, mid), BF16)] * 2
    inner = [pltpu.VMEM((rows * cols, 3 * depth), BF16)] * 2
    outer = [pltpu.VMEM(((rows + 4) * cols, 3 * depth), BF16)] * 2
    *image_parts, w_high, w_low = pl.pallas_call(
        first_prepare,
        out_shape=inner + weights,
        in_specs=[HBM] * 2,
        out_specs=[VMEM] * 4,
        scratch_shapes=[
            pltpu.VMEM((rows, cols, depth), F32),
            pltpu.VMEM((9, depth, mid), F32),
            pltpu.SemaphoreType.DMA((2,)),
        ],
        name="first_prepare",
        compiler_params=LIMIT,
    )(far(image_in), far(first_weight.reshape(9, depth, mid)))
    given, high, low = pl.pallas_call(
        first_given,
        out_shape=[pltpu.VMEM((half, mid), F32)] + outer,
        in_specs=[SMEM] + [VMEM] * 6,
        out_specs=[VMEM] * 3,
        name="first_given",
        compiler_params=LIMIT,
    )(core[None], *map(near, (above, below, *image_parts, w_high, w_low)))
    held = pl.pallas_call(
        functools.partial(first_held, cols),
        out_shape=pltpu.VMEM((half, mid), F32),
        in_specs=[SMEM] + [VMEM] * 4,
        out_specs=VMEM,
        name="first_held",
        compiler_params=LIMIT,
    )(core[None], *map(near, (high, low, w_high, w_low)))

    w_pair = pl.pallas_call(
        prepare,
        out_shape=pltpu.VMEM((3, 3 * mid, 2 * wide), BF16),
        in_specs=[VMEM],
        out_specs=VMEM,
        name="prepare",
        compiler_params=LIMIT,
    )(second_weight.reshape(9, mid, wide))

    held = held + lax.ppermute(given, "core", [(0, 1), (1, 0)])
    pieces = lax.all_to_all(held.reshape(chips, chunk, mid), "chip", 0, 0, tiled=True)
    grads = [out_grad]
    grads += [trade(grads[0], "slab", step) for step in STEPS[1:]]
    low_end = jnp.where(slab == 0, cols, 0)
    high_end = jnp.where(slab == slabs - 1, ext - cols, ext)
    own = pl.pallas_call(
        activate,
        out_shape=pltpu.VMEM((chunk, mid), F32),
        in_specs=[SMEM, VMEM],
        out_specs=VMEM,
        name="activate",
        compiler_params=LIMIT,
    )(jnp.stack([(core * chips + chip) * chunk, low_end, high_end]), near(pieces))
    hidden = lax.all_gather(own, ("chip", "core"), axis=0, tiled=False)

    lanes = 2 * mid // slabs
    count = rows * cols // 2
    conv, *local = pl.pallas_call(
        second_conv,
        out_shape=[pltpu.VMEM((n_out, rows, cols // n_out, wide), F32)]
        + [pltpu.VMEM((count, lanes), F32)] * slabs,
        in_specs=[SMEM] + [VMEM] * 2,
        out_specs=[VMEM] * (1 + slabs),
        scratch_shapes=[
            pltpu.VMEM((ext, mid), F32),
            pltpu.VMEM((ext, 3 * mid), BF16),
            pltpu.VMEM((ext, 3 * mid), BF16),
            pltpu.VMEM((slabs, count, lanes), F32),
        ],
        name="second_conv",
        compiler_params=LIMIT,
    )(slab[None], near(hidden), near(w_pair))

    gathered = lax.all_to_all(conv, "cout", 0, 0, tiled=True)
    local[1:] = [trade(local[k], "slab", STEPS[k]) for k in range(1, slabs)]
    pixels = rows * cols
    early = slabs // 2
    tap_pair = [pltpu.VMEM((early, pixels, 2 * lanes), BF16)] * 2
    sums, grad_last = pl.pallas_call(
        functools.partial(early_sums, cols),
        out_shape=[
            pltpu.VMEM((3, wide, 2 * lanes), F32),
            pltpu.VMEM((slabs - early, 3, 2 * wide, pixels), BF16),
        ],
        in_specs=[SMEM] + [HBM] * slabs + [VMEM] * early,
        out_specs=[VMEM] * 2,
        scratch_shapes=tap_pair
        + [
            pltpu.VMEM((early, 3, 2 * wide, pixels), BF16),
            pltpu.VMEM((slabs * rows + 2, cols, wide), F32),
            pltpu.SemaphoreType.DMA((slabs,)),
        ],
        name="early_sums",
        compiler_params=LIMIT,
    )(slab[None], *map(far, grads), *map(near, local[:early]))
    weight_grad, output = pl.pallas_call(
        functools.partial(last_sums, cols),
        out_shape=[
            jax.ShapeDtypeStruct((9, mid // slabs, wide), F32),
            jax.ShapeDtypeStruct((rows, cols // n_out, wide), F32),
        ],
        in_specs=[VMEM] * (slabs - early + 3),
        out_specs=[VMEM] * 2,
        scratch_shapes=tap_pair,
        name="last_sums",
        compiler_params=LIMIT,
    )(*map(near, (*local[early:], grad_last, sums, gathered)))
    weight_grad = weight_grad.reshape(3, 3, mid // slabs, wide)
    return (output, weight_grad)


def solution(mesh):
    cin = ("chip", "core")
    in_specs = (
        P("slab", None, cin),
        P(None, None, cin, "cout"),
        P(None, None, "cout", cin),
        P("slab", None, cin),
    )
    out_specs = (P("slab", "cout", cin), P(None, None, ("cout", "slab"), cin))
    slabs, n_out, n_in = mesh.devices.shape
    devices = mesh.devices.reshape(slabs, n_out, n_in // CORES, CORES)
    split_mesh = Mesh(devices, ("slab", "cout", *cin))
    return jax.shard_map(
        block, mesh=split_mesh, in_specs=in_specs, out_specs=out_specs, check_vma=False
    )
```

```python
import functools

import jax
import jax.numpy as jnp
from jax import lax
from jax.experimental import pallas as pl
from jax.experimental.pallas import tpu as pltpu
from jax.sharding import Mesh, PartitionSpec as P


F32, BF16 = jnp.float32, jnp.bfloat16
VMEM = pl.BlockSpec(memory_space=pltpu.VMEM)
HBM = pl.BlockSpec(memory_space=pltpu.HBM)
SMEM = pl.BlockSpec(memory_space=pltpu.SMEM)
CORES = 2
STEPS = (0, 2, 1, 3)
LIMIT = pltpu.CompilerParams(vmem_limit_bytes=24 * 2**20)


def near(value):
    return pltpu.with_memory_space_constraint(value, pltpu.VMEM)


def far(value):
    return pltpu.with_memory_space_constraint(value, pltpu.HBM)


def shift(value, axis, step):
    count = lax.axis_size(axis)
    pairs = [(i, i + step) for i in range(count) if 0 <= i + step < count]
    return lax.ppermute(value, axis, pairs)


def trade(value, axis, step):
    count = lax.axis_size(axis)
    return lax.ppermute(value, axis, [(i, i ^ step) for i in range(count)])


def split(value):
    high = value.astype(BF16)
    return high, (value - high.astype(F32)).astype(BF16)


def dot(left, right):
    return jnp.dot(left, right, preferred_element_type=F32)


def taps_of_row(row):
    count = row.shape[0]
    at = lax.broadcasted_iota(jnp.int32, row.shape, 0)
    left = jnp.where(at == 0, 0.0, pltpu.roll(row, 1, 0))
    right = jnp.where(at == count - 1, 0.0, pltpu.roll(row, count - 1, 0))
    return left, row, right


def store_taps(row, high, low, start):
    rows, width = row.shape
    for tap, value in enumerate(taps_of_row(row)):
        top, rest = split(value)
        high[start : start + rows, tap * width : (tap + 1) * width] = top
        low[start : start + rows, tap * width : (tap + 1) * width] = rest


def first_prepare(image, weight, high, low, w_high, w_low, image_at, weight_at, sems):
    fetch_image = pltpu.make_async_copy(image, image_at, sems.at[0])
    fetch_weight = pltpu.make_async_copy(weight, weight_at, sems.at[1])
    fetch_image.start()
    fetch_weight.start()
    fetch_image.wait()
    rows, cols, depth = image_at.shape
    for row in range(rows):
        store_taps(image_at[row], high, low, row * cols)
    fetch_weight.wait()
    for tap in range(9):
        top, rest = split(weight_at[tap])
        w_high[tap // 3, (tap % 3) * depth : (tap % 3 + 1) * depth, :] = top
        w_low[tap // 3, (tap % 3) * depth : (tap % 3 + 1) * depth, :] = rest


def half_conv(out, part, cols, high, low, w_high, w_low):
    half = out.shape[0]
    total = None
    for a in range(3):
        rows = pl.ds(pl.multiple_of(part * half + a * cols, cols), half)
        term = dot(high[rows, :], w_high[a])
        term += dot(low[rows, :], w_high[a])
        term += dot(high[rows, :], w_low[a])
        total = term if total is None else total + term
    out[...] = total


def first_given(core, above, below, high_in, low_in, w_high, w_low, given, high, low):
    edge, cols, _ = above.shape
    inner = high_in.shape[0]
    high[edge * cols : edge * cols + inner, :] = high_in[...]
    low[edge * cols : edge * cols + inner, :] = low_in[...]
    for row in range(edge):
        store_taps(above[row], high, low, row * cols)
        store_taps(below[row], high, low, (edge + row) * cols + inner)
    half_conv(given, 1 - core[0], cols, high, low, w_high, w_low)


def first_held(cols, core, high, low, w_high, w_low, held):
    half_conv(held, core[0], cols, high, low, w_high, w_low)


def prepare(weight, w_pair):
    depth, wide = weight.shape[1], weight.shape[2]
    for tap in range(9):
        top, rest = split(weight[tap])
        w_pair[tap // 3, (tap % 3) * depth : (tap % 3 + 1) * depth, :wide] = top
        w_pair[tap // 3, (tap % 3) * depth : (tap % 3 + 1) * depth, wide:] = rest


def activate(ends, pieces, own):
    total = pieces[0]
    for piece in range(1, pieces.shape[0]):
        total += pieces[piece]
    pixel = ends[0] + lax.broadcasted_iota(jnp.int32, total.shape, 0)
    inside = (pixel >= ends[1]) & (pixel < ends[2])
    own[...] = jnp.where(inside, total / (1.0 + jnp.exp(-total)), 0.0)


def lower_lanes(shape):
    return lax.broadcasted_iota(jnp.int32, shape, 1) < shape[1] // 2


def swap_lanes(value):
    return pltpu.roll(value, value.shape[1] // 2, 1)


def second_conv(slab, hidden, w_pair, conv, *rest):
    *local, ordered, high, low, packed = rest
    n_in, chunk, _ = hidden.shape
    chips = n_in // CORES
    n_out, rows, width, wide = conv.shape
    cols = n_out * width
    for core in range(CORES):
        for chip in range(chips):
            start = (core * chips + chip) * chunk
            ordered[start : start + chunk, :] = hidden[chip * CORES + core]
    count, lanes = local[0].shape
    for quarter in range(len(local)):
        at = slice(quarter // 2 * lanes, (quarter // 2 + 1) * lanes)
        first = ordered[cols : cols + count, at]
        second = ordered[cols + count : cols + 2 * count, at]
        if quarter % 2:
            first = swap_lanes(first)
        else:
            second = swap_lanes(second)
        packed[quarter] = jnp.where(lower_lanes(first.shape), first, second)
    for step, out in zip(STEPS, local, strict=True):
        out[...] = packed[slab[0] ^ step]
    for row in range(rows + 2):
        store_taps(ordered[row * cols : (row + 1) * cols, :], high, low, row * cols)
    pixels = rows * cols
    main = None
    other = None
    for a in range(3):
        window = slice(a * cols, a * cols + pixels)
        one = dot(high[window, :], w_pair[a])
        two = dot(low[window, :], w_pair[a, :, :wide])
        main = one if main is None else main + one
        other = two if other is None else other + two
    total = main[:, :wide] + main[:, wide:] + other
    for row in range(rows):
        for block in range(n_out):
            start = row * cols + block * width
            conv[block, row] = total[start : start + width, :]


def pixel_taps(cols, source, high, low):
    count, lanes = source.shape
    for row in range(count // cols):
        left, here, right = taps_of_row(source[row * cols : (row + 1) * cols, :])
        lower = lower_lanes(here.shape)
        pairs = (
            (jnp.where(lower, left, swap_lanes(here)), right),
            (jnp.where(lower, swap_lanes(left), here), swap_lanes(right)),
        )
        for half, pair in enumerate(pairs):
            at = slice(half * count + row * cols, half * count + (row + 1) * cols)
            for k, value in enumerate(pair):
                top, rest = split(value)
                high[at, k * lanes : (k + 1) * lanes] = top
                low[at, k * lanes : (k + 1) * lanes] = rest


def pixel_sums(grad_t, high, low):
    wide = grad_t.shape[1] // 2
    sums = []
    for a in range(3):
        both = dot(grad_t[a], high[...])
        sums.append(both[:wide] + both[wide:] + dot(grad_t[a, :wide, :], low[...]))
    return sums


def early_sums(cols, slab, *refs):
    *refs, out, grad_last, high, low, grad_t, whole, sems = refs
    slabs = sems.shape[0]
    grads, local = refs[:slabs], refs[slabs:]
    rows, _, wide = grads[0].shape
    early = len(local)
    copies = []
    for step, grad in enumerate(grads):
        into = whole.at[pl.ds(1 + (slab[0] ^ STEPS[step]) * rows, rows)]
        copies.append(pltpu.make_async_copy(grad, into, sems.at[step]))
        copies[step].start()
    blank = jnp.zeros((cols, wide), F32)
    whole[0] = blank
    whole[whole.shape[0] - 1] = blank
    for step, source in enumerate(local):
        pixel_taps(cols, source, high.at[step], low.at[step])
    for copy in copies:
        copy.wait()
    for step in range(slabs):
        into = grad_t.at[step] if step < early else grad_last.at[step - early]
        for a in range(3):
            window = whole[pl.ds((slab[0] ^ STEPS[step]) * rows + 2 - a, rows)]
            top, rest = split(window.reshape(rows * cols, wide).T)
            into[a, :wide, :] = top
            into[a, wide:, :] = rest
    for step in range(early):
        sums = pixel_sums(grad_t.at[step], high.at[step], low.at[step])
        for a, value in enumerate(sums):
            out[a] = value if step == 0 else out[a] + value


def middle_sums(cols, source, grad_t, sums, out, high, low):
    pixel_taps(cols, source, high, low)
    for a, value in enumerate(pixel_sums(grad_t.at[0], high, low)):
        out[a] = sums[a] + value


def last_sums(cols, *refs):
    *local, grad_t, sums, gathered, out, output, high, low = refs
    part = out.shape[1]
    terms = []
    for step, source in enumerate(local):
        pixel_taps(cols, source, high.at[step], low.at[step])
        terms.append(pixel_sums(grad_t.at[step + 1], high.at[step], low.at[step]))
    for a in range(3):
        turned = sum((term[a] for term in terms), sums[a]).T
        for b in range(3):
            out[a * 3 + b] = turned[b * part : (b + 1) * part, :]
    total = gathered[0]
    for piece in range(1, gathered.shape[0]):
        total += gathered[piece]
    output[...] = total


def block(image_in, first_weight, second_weight, out_grad):
    rows, cols, depth = image_in.shape
    mid = first_weight.shape[3]
    wide = second_weight.shape[3]
    slabs, chips, n_out = lax.axis_size("slab"), lax.axis_size("chip"), lax.axis_size("cout")
    slab, chip, core = lax.axis_index("slab"), lax.axis_index("chip"), lax.axis_index("core")
    ext = (rows + 2) * cols
    half = ext // CORES
    chunk = half // chips

    above = shift(image_in[rows - 2 :], "slab", 1)
    below = shift(image_in[:2], "slab", -1)
    weights = [pltpu.VMEM((3, 3 * depth, mid), BF16)] * 2
    inner = [pltpu.VMEM((rows * cols, 3 * depth), BF16)] * 2
    outer = [pltpu.VMEM(((rows + 4) * cols, 3 * depth), BF16)] * 2
    *image_parts, w_high, w_low = pl.pallas_call(
        first_prepare,
        out_shape=inner + weights,
        in_specs=[HBM] * 2,
        out_specs=[VMEM] * 4,
        scratch_shapes=[
            pltpu.VMEM((rows, cols, depth), F32),
            pltpu.VMEM((9, depth, mid), F32),
            pltpu.SemaphoreType.DMA((2,)),
        ],
        name="first_prepare",
        compiler_params=LIMIT,
    )(far(image_in), far(first_weight.reshape(9, depth, mid)))
    given, high, low = pl.pallas_call(
        first_given,
        out_shape=[pltpu.VMEM((half, mid), F32)] + outer,
        in_specs=[SMEM] + [VMEM] * 6,
        out_specs=[VMEM] * 3,
        name="first_given",
        compiler_params=LIMIT,
    )(core[None], *map(near, (above, below, *image_parts, w_high, w_low)))
    held = pl.pallas_call(
        functools.partial(first_held, cols),
        out_shape=pltpu.VMEM((half, mid), F32),
        in_specs=[SMEM] + [VMEM] * 4,
        out_specs=VMEM,
        name="first_held",
        compiler_params=LIMIT,
    )(core[None], *map(near, (high, low, w_high, w_low)))

    w_pair = pl.pallas_call(
        prepare,
        out_shape=pltpu.VMEM((3, 3 * mid, 2 * wide), BF16),
        in_specs=[VMEM],
        out_specs=VMEM,
        name="prepare",
        compiler_params=LIMIT,
    )(second_weight.reshape(9, mid, wide))

    held = held + lax.ppermute(given, "core", [(0, 1), (1, 0)])
    pieces = lax.all_to_all(held.reshape(chips, chunk, mid), "chip", 0, 0, tiled=True)
    grads = [out_grad]
    grads += [trade(grads[0], "slab", step) for step in STEPS[1:]]
    low_end = jnp.where(slab == 0, cols, 0)
    high_end = jnp.where(slab == slabs - 1, ext - cols, ext)
    own = pl.pallas_call(
        activate,
        out_shape=pltpu.VMEM((chunk, mid), F32),
        in_specs=[SMEM, VMEM],
        out_specs=VMEM,
        name="activate",
        compiler_params=LIMIT,
    )(jnp.stack([(core * chips + chip) * chunk, low_end, high_end]), near(pieces))
    hidden = lax.all_gather(own, ("chip", "core"), axis=0, tiled=False)

    lanes = 2 * mid // slabs
    count = rows * cols // 2
    conv, *local = pl.pallas_call(
        second_conv,
        out_shape=[pltpu.VMEM((n_out, rows, cols // n_out, wide), F32)]
        + [pltpu.VMEM((count, lanes), F32)] * slabs,
        in_specs=[SMEM] + [VMEM] * 2,
        out_specs=[VMEM] * (1 + slabs),
        scratch_shapes=[
            pltpu.VMEM((ext, mid), F32),
            pltpu.VMEM((ext, 3 * mid), BF16),
            pltpu.VMEM((ext, 3 * mid), BF16),
            pltpu.VMEM((slabs, count, lanes), F32),
        ],
        name="second_conv",
        compiler_params=LIMIT,
    )(slab[None], near(hidden), near(w_pair))

    gathered = lax.all_to_all(conv, "cout", 0, 0, tiled=True)
    local[1:] = [trade(local[k], "slab", STEPS[k]) for k in range(1, slabs)]
    pixels = rows * cols
    early = slabs // 2
    tap_pair = [pltpu.VMEM((early, pixels, 2 * lanes), BF16)] * 2
    sums, grad_last = pl.pallas_call(
        functools.partial(early_sums, cols),
        out_shape=[
            pltpu.VMEM((3, wide, 2 * lanes), F32),
            pltpu.VMEM((slabs - early, 3, 2 * wide, pixels), BF16),
        ],
        in_specs=[SMEM] + [HBM] * slabs + [VMEM] * early,
        out_specs=[VMEM] * 2,
        scratch_shapes=tap_pair
        + [
            pltpu.VMEM((early, 3, 2 * wide, pixels), BF16),
            pltpu.VMEM((slabs * rows + 2, cols, wide), F32),
            pltpu.SemaphoreType.DMA((slabs,)),
        ],
        name="early_sums",
        compiler_params=LIMIT,
    )(slab[None], *map(far, grads), *map(near, local[:early]))
    sums = pl.pallas_call(
        functools.partial(middle_sums, cols),
        out_shape=pltpu.VMEM((3, wide, 2 * lanes), F32),
        in_specs=[VMEM] * 3,
        out_specs=VMEM,
        scratch_shapes=[pltpu.VMEM((pixels, 2 * lanes), BF16)] * 2,
        name="middle_sums",
        compiler_params=LIMIT,
    )(*map(near, (local[early], grad_last, sums)))
    weight_grad, output = pl.pallas_call(
        functools.partial(last_sums, cols),
        out_shape=[
            jax.ShapeDtypeStruct((9, mid // slabs, wide), F32),
            jax.ShapeDtypeStruct((rows, cols // n_out, wide), F32),
        ],
        in_specs=[VMEM] * (slabs - early + 2),
        out_specs=[VMEM] * 2,
        scratch_shapes=tap_pair,
        name="last_sums",
        compiler_params=LIMIT,
    )(*map(near, (*local[early + 1 :], grad_last, sums, gathered)))
    weight_grad = weight_grad.reshape(3, 3, mid // slabs, wide)
    return (output, weight_grad)


def solution(mesh):
    cin = ("chip", "core")
    in_specs = (
        P("slab", None, cin),
        P(None, None, cin, "cout"),
        P(None, None, "cout", cin),
        P("slab", None, cin),
    )
    out_specs = (P("slab", "cout", cin), P(None, None, ("cout", "slab"), cin))
    slabs, n_out, n_in = mesh.devices.shape
    devices = mesh.devices.reshape(slabs, n_out, n_in // CORES, CORES)
    split_mesh = Mesh(devices, ("slab", "cout", *cin))
    return jax.shard_map(
        block, mesh=split_mesh, in_specs=in_specs, out_specs=out_specs, check_vma=False
    )
```
